1024 devices in a mesh: section: 4 (over y_lo), expert: 64 (over z, x), dp: 4 (over y_hi, core).
Axes of the slice: x: 8, y: 8 (y_hi: 2, y_lo: 4; y = y_hi * 4 + y_lo), z: 8, core: 2. Of those that a mesh axis runs over, the one named last changes fastest.
Arguments:
- upstream: bfloat16 [32768, 2048], P(('expert', 'dp')), may hold values from -6 to 6
- expert_ids: int32 [32768, 2], P(('expert', 'dp')), may hold values from 0 to 255, all different within a row; in each aligned block of 128 rows (0 to 127, 128 to 255, ...) at most 2 rows name the same one
- gate_index: int32 [32768, 2], P(('expert', 'dp')), may hold values from 0 to 63
- gate_table: float32 [64], replicated, may hold values from 0.1 to 1
- w_up: bfloat16 [256, 2048, 1408], P(('expert', 'dp'), 'section'), may hold values from -0.125 to 0.125
- w_down: bfloat16 [256, 1408, 2048], P(('expert', 'dp'), 'section'), may hold values from -0.15625 to 0.15625
- saved_pre: bfloat16 [256, 256, 2, 1408], P(('expert', 'dp'), None, None, 'section'), may hold values from -6 to 6
Outputs:
- grad_input: bfloat16 [32768, 2048], P(('expert', 'dp'), 'section')
The draws below stay inside these ranges and needn't reach their ends.
Inputs may be any that keep to these rules, and one draw needn't show every extreme that they name: `expert_ids`: A token's 2 experts are different; within each aligned block of 128 tokens no expert is named more than 2 times, a bound that some block reaches.
All inputs are finite; a program needn't handle non-finite values.
Results may differ from the reference program's by a relative error of at most 0.0044.
Values may be sent and summed in bfloat16 or wider, within the bound.
No kernel may reach another device: no remote copies, remote signals or barrier semaphores. Data moves between devices by JAX's collectives and lax.ppermute only.
A program may use at most 32 MiB of HBM per device.

```python
import math
import jax
import jax.numpy as jnp
import numpy as np
from jax import lax

D = 2048
FF = 1408
TOP = 2
LEVELS = 64
TOK_DEV = 128
EXPERTS = 256
SOURCES = 256
CAP = 2
TOKENS = 32768


def place_ends(array, own_key, least, top_value):
    longest = array.shape.index(max(array.shape))
    spots = []
    for shift in (0, 1):
        where = [jax.random.randint(jax.random.fold_in(own_key, axis), (), 0, length) for axis, length in enumerate(array.shape)]
        where[longest] = (where[longest] + shift) % array.shape[longest]
        spots.append(tuple(where))
    return array.at[spots[0]].set(least).at[spots[1]].set(top_value)


def block_scale(stream_key, extent, cuts, least, high):
    factor_of, own = 1.0, jax.random.fold_in(stream_key, 6)
    for position, blocks in cuts:
        steps = jnp.exp(jax.random.uniform(jax.random.fold_in(own, position), (blocks,), jnp.float32, least / len(cuts), high / len(cuts)))
        factor_of = factor_of * jnp.repeat(steps, extent[position] // blocks).reshape([-1 if axis == position else 1 for axis in range(len(extent))])
    return factor_of


def assign_block(key, own, number, rows, amount, top, limit, lean):
    sequence = jax.random.permutation(key, amount)
    packed, usual = portions_of(amount, rows * top, limit, lean, True), portions_of(amount, rows * top, limit, lean, False)
    places = jnp.arange(amount)

    def named(lengths, turn):
        used = int((lengths > 0).sum())
        fixed = max(1, used // 4)
        shifted = fixed + (places - fixed + turn * (used - fixed)) % max(1, amount - fixed)
        return jnp.zeros((amount,), jnp.int32).at[sequence[jnp.where(places < fixed, places, shifted)]].set(jnp.asarray(lengths, jnp.int32))

    lengths = jnp.where(number % 4 == 0, named(packed, number // 4), named(usual, number - number // 4 - 1))
    mixed = jax.random.permutation(jax.random.fold_in(own, 3), amount)
    source_of, receiver = mixed[0:amount // 2 * 2:2], mixed[1:amount // 2 * 2:2]
    slack = jnp.minimum(lengths[source_of] - 1, limit - lengths[receiver]) // 2
    slack = jnp.where((source_of == sequence[0]) | (receiver == sequence[0]) | (lengths[receiver] == 0), 0, jnp.maximum(slack, 0))
    shifted = jax.random.randint(jax.random.fold_in(own, 4), (amount // 2,), 0, 1 << 20) % (slack + 1)
    lengths = lengths.at[source_of].add(-shifted).at[receiver].add(shifted)
    items = jnp.searchsorted(jnp.cumsum(lengths), jnp.arange(rows * top), side="right").astype(jnp.int32)
    table = items.reshape(top, rows).T
    table = table[jax.random.permutation(jax.random.fold_in(own, 1), rows)]
    turn = jax.random.randint(jax.random.fold_in(own, 2), (rows, 1), 0, top)
    return jnp.take_along_axis(table, (jnp.arange(top)[None, :] + turn) % top, axis=1)


def portions_of(amount, total, most, slope, full):
    loads = [(1 << 20) // math.isqrt(standing ** slope) + 1 for standing in range(1, amount + 1)]
    largest = most if full else min(most, max(-(-total // amount), total * loads[0] // sum(loads)))
    least = 1 if total - largest >= amount - 1 else 0
    holding, surplus = [largest] + [least] * (amount - 1), total - largest - least * (amount - 1)
    while surplus > 0:
        free = [i for i in range(1, amount) if holding[i] < largest] or [i for i in range(1, amount) if holding[i] < most]
        mass, left = sum([loads[i] for i in free]), surplus
        for i in free:
            addition = min(most - holding[i], max(1, left * loads[i] // mass), surplus)
            holding[i] = holding[i] + addition
            surplus = surplus - addition
    return np.array(holding)


def centred(stream_key, dims, deviation, most, pieces=(), kind=jnp.bfloat16):
    array = deviation * jax.random.normal(stream_key, dims, jnp.float32)
    if pieces:
        array = array * block_scale(stream_key, dims, pieces, -0.22, 0.18)
    return jnp.clip(array, -most, most).astype(kind)


def setup_inputs(seed: int = 0) -> dict:
    streams_of = jax.random.split(jax.random.key(seed), 8)
    upstream = centred(streams_of[0], (TOKENS, D), 1.0, 6.0, ((0, 256),))
    expert_ids_keys = jax.random.split(jax.random.fold_in(streams_of[1], 1), TOKENS // TOK_DEV)
    expert_ids_turns = jax.random.permutation(jax.random.fold_in(streams_of[1], 3), TOKENS // TOK_DEV)
    expert_ids = jax.vmap(lambda own, number: assign_block(jax.random.fold_in(streams_of[1], 2), own, number, TOK_DEV, EXPERTS, TOP, CAP, 2))(expert_ids_keys, expert_ids_turns).reshape((TOKENS, TOP))
    gate_index = place_ends(jax.random.randint(streams_of[2], (TOKENS, TOP), 0, LEVELS), jax.random.fold_in(streams_of[2], 1), 0, LEVELS - 1).astype(jnp.int32)
    gate_table = jnp.clip(jnp.exp(jax.random.uniform(streams_of[3], (LEVELS,), jnp.float32, math.log(0.1), math.log(1.0))), 0.1, 1.0)
    w_up = centred(streams_of[4], (EXPERTS, D, FF), D ** -0.5, 0.125, ((0, 256), (1, 4)))
    w_down = centred(streams_of[5], (EXPERTS, FF, D), FF ** -0.5, 0.15625, ((0, 256), (1, 4)))
    saved_pre = centred(streams_of[6], (EXPERTS, SOURCES, CAP, FF), 1.5, 6.0, ((0, 256), (3, 4)))
    return dict(upstream=upstream, expert_ids=expert_ids, gate_index=gate_index, gate_table=gate_table, w_up=w_up, w_down=w_down, saved_pre=saved_pre)


def dsilu_of(pre_act):
    sig_value = jax.nn.sigmoid(pre_act)
    return sig_value * (1.0 + pre_act * (1.0 - sig_value))


def slot_places(ids_block):
    chosen = (ids_block[:, :, None] == jnp.arange(EXPERTS, dtype=jnp.int32)).astype(jnp.int32)
    per_token = jnp.sum(chosen, axis=1).astype(jnp.int32)
    earlier = (jnp.cumsum(per_token, axis=0) - per_token).astype(jnp.int32)
    ranks = jnp.sum(chosen * earlier[:, None, :], axis=2).astype(jnp.int32)
    return (ids_block * CAP + ranks).astype(jnp.int32)


def expert_rows(operands):
    rows, pre_act, up_weight, down_weight = operands
    proj_grad = jnp.dot(rows, down_weight.T, preferred_element_type=jnp.float32)
    hid_grad = (proj_grad * dsilu_of(pre_act.astype(jnp.float32))).astype(jnp.bfloat16)
    return jnp.dot(hid_grad, up_weight.T, preferred_element_type=jnp.float32).astype(jnp.bfloat16)


def build_buffer(place_block, rows_block):
    empty = jnp.zeros((EXPERTS * CAP, D), jnp.bfloat16)
    return empty.at[place_block.reshape(-1)].set(rows_block.reshape(-1, D))


def pick_rows(table_rows, place_block):
    return table_rows[place_block]


def reference(upstream, expert_ids, gate_index, gate_table, w_up, w_down, saved_pre):
    grad_blocks = upstream.reshape(SOURCES, TOK_DEV, D)
    id_blocks = expert_ids.reshape(SOURCES, TOK_DEV, TOP)
    places = jax.vmap(slot_places)(id_blocks)
    gate_values = gate_table[gate_index].reshape(SOURCES, TOK_DEV, TOP)
    sent_rows = (gate_values[:, :, :, None] * grad_blocks.astype(jnp.float32)[:, :, None, :]).astype(jnp.bfloat16)
    buffers = jax.vmap(build_buffer)(places, sent_rows)
    received = buffers.reshape(SOURCES, EXPERTS, CAP, D).transpose(1, 0, 2, 3).reshape(EXPERTS, SOURCES * CAP, D)
    back_rows = lax.map(expert_rows, (received, saved_pre.reshape(EXPERTS, SOURCES * CAP, FF), w_up, w_down))
    returned = back_rows.reshape(EXPERTS, SOURCES, CAP, D).transpose(1, 0, 2, 3).reshape(SOURCES, EXPERTS * CAP, D)
    picked = jax.vmap(pick_rows)(returned, places)
    result = grad_blocks.astype(jnp.float32) + jnp.sum(picked.astype(jnp.float32), axis=2)
    return result.astype(jnp.bfloat16).reshape(TOKENS, D)
```

```python
import jax
import jax.numpy as jnp
from jax import lax
from jax.sharding import PartitionSpec as P

NEAR = [(0, 1), (1, 0), (2, 3), (3, 2)]
FAR = [(0, 2), (2, 0), (1, 3), (3, 1)]
CROSS = [((3, 0), (0, 1)), ((0, 1), (3, 0)), ((0, 0), (2, 1)), ((3, 1), (1, 0))]


def cross_pairs():
    pairs = []
    for (s0, h0), (s1, h1) in CROSS:
        for core in range(2):
            pairs.append((s0 * 4 + h0 * 2 + core, s1 * 4 + h1 * 2 + core))
    return pairs


def ranks_of(flat_ids, tokens):
    pair = jnp.arange(flat_ids.shape[0], dtype=jnp.int32)
    token = jnp.where(pair >= tokens, pair - tokens, pair)
    same = (flat_ids[:, None] == flat_ids[None, :]) & (token[:, None] < token[None, :])
    return jnp.sum(same.astype(jnp.int32), axis=0)


def body(upstream, expert_ids, gate_index, gate_table, w_up, w_down, saved_pre):
    tokens, model_width = upstream.shape
    col_part = model_width // lax.axis_size("section")
    groups = lax.axis_size("expert")
    levels = gate_table.shape[0]
    capacity = saved_pre.shape[2]
    hidden_part = w_down.shape[1]
    section = lax.axis_index("section")
    member = lax.axis_index("dp")
    half = member // 2
    kind = section % 2
    hidden_pair = section // 2
    slots = groups * 2 * capacity

    weight_own = w_down[0]
    weight_other = lax.ppermute(weight_own, "section", NEAR)
    pre = saved_pre[0].reshape(groups, 2, 2, capacity, hidden_part)
    pre_mine = jnp.where(kind == 0, pre[:, 0], pre[:, 1]).reshape(slots, hidden_part)
    pre_theirs = jnp.where(kind == 0, pre[:, 1], pre[:, 0]).reshape(slots, hidden_part)
    pre_mine = pre_mine.T
    pre_other = lax.ppermute(pre_theirs.T, "section", NEAR)

    packed = expert_ids.T * levels + gate_index.T
    crossing = kind != half
    packed_in = lax.ppermute(packed, ("section", "dp"), cross_pairs())
    block_in = lax.ppermute(upstream, ("section", "dp"), cross_pairs())
    served = jnp.where(crossing, packed_in, packed).reshape(-1)
    block = jnp.where(crossing, block_in, upstream)

    ids = served // levels
    gates = jnp.sum(
        jnp.where(
            (served % levels)[None, :] == jnp.arange(levels, dtype=jnp.int32)[:, None],
            gate_table[:, None],
            0.0,
        ),
        axis=0,
    )
    here = (ids % 4) // 2 == half
    row = jnp.where(here, ((ids // 4) * 2 + ids % 2) * capacity + ranks_of(ids, tokens), -1)
    match = row[None, :] == jnp.arange(slots, dtype=jnp.int32)[:, None]
    row_gate = jnp.sum(jnp.where(match, gates[None, :], 0.0), axis=1)
    chosen = (match[:, :tokens] | match[:, tokens:]).astype(jnp.bfloat16)
    picked = jnp.dot(chosen, block, preferred_element_type=jnp.float32)
    rows = (row_gate[:, None] * picked).astype(jnp.bfloat16)
    halves = [[g * 4 + h * 2 + c for g in range(groups) for c in range(2)] for h in range(2)]
    arrived = lax.all_to_all(
        rows.reshape(groups * 2, capacity, model_width),
        ("expert", "dp"),
        split_axis=0,
        concat_axis=0,
        axis_index_groups=halves,
        tiled=True,
    ).reshape(slots, model_width)

    def hidden_grad(weight, pre_act):
        proj = jnp.einsum("fd,sd->fs", weight, arrived, preferred_element_type=jnp.float32)
        pre_act = pre_act.astype(jnp.float32)
        sig = jax.nn.sigmoid(pre_act)
        return (proj * (sig * (1.0 + pre_act * (1.0 - sig)))).astype(jnp.bfloat16)

    hid_own = hidden_grad(weight_own, pre_mine)
    hid_other = hidden_grad(weight_other, pre_other)
    hid = jnp.concatenate(
        [jnp.where(kind == 0, hid_own, hid_other), jnp.where(kind == 0, hid_other, hid_own)]
    )
    far = lax.ppermute(hid, "section", FAR)
    near = lax.ppermute(hid, "section", NEAR)
    far_near = lax.ppermute(far, "section", NEAR)

    def back(own_pair, other_pair):
        whole = jnp.concatenate(
            [
                jnp.where(hidden_pair == 0, own_pair, other_pair),
                jnp.where(hidden_pair == 0, other_pair, own_pair),
            ]
        )
        out = jnp.einsum("fs,df->sd", whole, w_up[0], preferred_element_type=jnp.float32)
        return out.astype(jnp.bfloat16).reshape(groups, 2, capacity, col_part)

    mine, theirs = back(hid, far), back(near, far_near)
    back_rows = jnp.stack(
        [jnp.where(kind == 0, mine, theirs), jnp.where(kind == 0, theirs, mine)], axis=1
    ).reshape(groups * 4, capacity, col_part)
    returned = lax.all_to_all(
        back_rows, ("expert", "dp"), split_axis=0, concat_axis=0, tiled=True
    ).reshape(groups * 4 * capacity, col_part)

    flat_ids = expert_ids.T.reshape(-1)
    places = flat_ids * capacity + ranks_of(flat_ids, tokens)
    wanted = places[:, None] == jnp.arange(groups * 4 * capacity, dtype=jnp.int32)
    wanted = (wanted[:tokens] | wanted[tokens:]).astype(jnp.bfloat16)
    total = jnp.dot(wanted, returned, preferred_element_type=jnp.float32)
    own_cols = lax.dynamic_slice_in_dim(upstream, section * col_part, col_part, 1)
    return (own_cols.astype(jnp.float32) + total).astype(jnp.bfloat16)


def solution(mesh):
    in_specs = (
        P(("expert", "dp"), None),
        P(("expert", "dp"), None),
        P(("expert", "dp"), None),
        P(),
        P(("expert", "dp"), "section", None),
        P(("expert", "dp"), "section", None),
        P(("expert", "dp"), None, None, "section"),
    )
    out_specs = P(("expert", "dp"), "section")
    return jax.shard_map(body, mesh=mesh, in_specs=in_specs, out_specs=out_specs, check_vma=False)
```

```python
import jax
import jax.numpy as jnp
from jax import lax
from jax.experimental import pallas as pl
from jax.experimental.pallas import tpu as pltpu
from jax.sharding import PartitionSpec as P

NEAR = [(0, 1), (1, 0), (2, 3), (3, 2)]
FAR = [(0, 2), (2, 0), (1, 3), (3, 1)]
HELD_FLOPS = 100_000_000_000


def held(array):
    def kernel(source, target):
        del source, target

    return pl.pallas_call(
        kernel,
        out_shape=jax.ShapeDtypeStruct(array.shape, array.dtype),
        in_specs=[pl.BlockSpec(memory_space=pl.ANY)],
        out_specs=pl.BlockSpec(memory_space=pl.ANY),
        input_output_aliases={0: 0},
        cost_estimate=pl.CostEstimate(flops=HELD_FLOPS, bytes_accessed=0, transcendentals=0),
        name="held",
    )(array)


def mirrored_groups(groups):
    def device(s, g, half, core):
        return ((s if half == 0 else 3 - s) * groups + g) * 4 + half * 2 + core

    return [
        [device(s, g, h, c) for g in range(groups) for h in range(2) for c in range(2)]
        for s in range(4)
    ]


def ranks_of(flat_ids, tokens):
    pair = jnp.arange(flat_ids.shape[0], dtype=jnp.int32)
    token = jnp.where(pair >= tokens, pair - tokens, pair)
    same = (flat_ids[:, None] == flat_ids[None, :]) & (token[:, None] < token[None, :])
    return jnp.sum(same.astype(jnp.int32), axis=0)


def body(upstream, expert_ids, gate_index, gate_table, w_up, w_down, saved_pre):
    tokens, model_width = upstream.shape
    col_part = model_width // lax.axis_size("section")
    groups = lax.axis_size("expert")
    experts = groups * lax.axis_size("dp")
    levels = gate_table.shape[0]
    capacity = saved_pre.shape[2]
    hidden_part = w_down.shape[1]
    section = lax.axis_index("section")
    half = lax.axis_index("dp") // 2
    first = section % 2 == 0
    kind = jnp.where(first, half, 1 - half)
    hidden_pair = section // 2

    flat_ids = expert_ids.T.reshape(-1)
    flat_index = gate_index.T.reshape(-1)
    ranks = ranks_of(flat_ids, tokens)
    gates = jnp.sum(
        jnp.where(
            flat_index[None, :] == jnp.arange(levels, dtype=jnp.int32)[:, None],
            gate_table[:, None],
            0.0,
        ),
        axis=0,
    )
    row = jnp.where(ranks == kind, flat_ids, -1)
    match = row[None, :] == jnp.arange(experts, dtype=jnp.int32)[:, None]
    row_gate = jnp.sum(jnp.where(match, gates[None, :], 0.0), axis=1)
    chosen = (match[:, :tokens] | match[:, tokens:]).astype(jnp.bfloat16)
    picked = jnp.dot(chosen, upstream, preferred_element_type=jnp.float32)
    rows = (row_gate[:, None] * picked).astype(jnp.bfloat16)
    arrived = lax.all_to_all(
        rows.reshape(experts, 2, model_width // 2),
        ("section", "expert", "dp"),
        split_axis=0,
        concat_axis=0,
        axis_index_groups=mirrored_groups(groups),
        tiled=True,
    ).reshape(experts, model_width)

    weight_own = w_down[0]
    weight_other = held(lax.ppermute(weight_own, "section", NEAR))
    pre = saved_pre[0].transpose(1, 2, 0)
    pre_mine = jnp.where(kind == 0, pre[0], pre[1])
    pre_other = lax.ppermute(jnp.where(kind == 0, pre[1], pre[0]), "section", NEAR)

    def hidden_grad(weight, pre_act):
        proj = jnp.einsum("fd,sd->fs", weight, arrived, preferred_element_type=jnp.float32)
        pre_act = pre_act.astype(jnp.float32)
        sig = jax.nn.sigmoid(pre_act)
        return (proj * (sig * (1.0 + pre_act * (1.0 - sig)))).astype(jnp.bfloat16)

    hid_own = hidden_grad(weight_own, pre_mine)
    far_own = lax.ppermute(hid_own, "section", FAR)
    near_own = lax.ppermute(hid_own, "section", NEAR)
    hid_other = hidden_grad(weight_other, pre_other)
    far_other = lax.ppermute(hid_other, "section", FAR)
    near_other = lax.ppermute(hid_other, "section", NEAR)
    relay_own = lax.ppermute(far_own, "section", NEAR)
    relay_other = lax.ppermute(far_other, "section", NEAR)

    pairs = w_up[0].reshape(col_part, 2, 2 * hidden_part)
    pairs = jnp.where(hidden_pair == 0, pairs, pairs[:, ::-1])
    parts = pairs.reshape(col_part, 2, 2, hidden_part)
    parts = jnp.where(first, parts, parts[:, :, ::-1]).reshape(col_part, 4 * hidden_part)

    def back(pieces):
        out = jnp.einsum(
            "fs,df->sd", jnp.concatenate(pieces), parts, preferred_element_type=jnp.float32
        )
        return out.astype(jnp.bfloat16)

    mine = back([hid_own, hid_other, far_own, far_other])
    theirs = back([near_other, near_own, relay_other, relay_own])
    back_rows = jnp.stack([mine, theirs], axis=1)
    returned = lax.all_to_all(
        back_rows, ("expert", "dp"), split_axis=0, concat_axis=0, tiled=True
    ).reshape(experts * capacity, col_part)

    sender_half = (flat_ids % 4) // 2
    served = jnp.where(first, sender_half, 1 - sender_half)
    places = flat_ids * capacity + jnp.where(ranks == served, 0, 1)
    wanted = places[:, None] == jnp.arange(experts * capacity, dtype=jnp.int32)
    wanted = (wanted[:tokens] | wanted[tokens:]).astype(jnp.bfloat16)
    total = jnp.dot(wanted, returned, preferred_element_type=jnp.float32)
    own_cols = lax.dynamic_slice_in_dim(upstream, section * col_part, col_part, 1)
    return (own_cols.astype(jnp.float32) + total).astype(jnp.bfloat16)


def solution(mesh):
    in_specs = (
        P(("expert", "dp"), None),
        P(("expert", "dp"), None),
        P(("expert", "dp"), None),
        P(),
        P(("expert", "dp"), "section", None),
        P(("expert", "dp"), "section", None),
        P(("expert", "dp"), None, None, "section"),
    )
    out_specs = P(("expert", "dp"), "section")
    return jax.shard_map(body, mesh=mesh, in_specs=in_specs, out_specs=out_specs, check_vma=False)
```

```python
import jax
import jax.numpy as jnp
from jax import lax
from jax.experimental import pallas as pl
from jax.experimental.pallas import tpu as pltpu
from jax.sharding import PartitionSpec as P

NEAR = [(0, 1), (1, 0), (2, 3), (3, 2)]
FAR = [(0, 2), (2, 0), (1, 3), (3, 1)]
HELD_FLOPS = 100_000_000_000


def held(array, flops):
    def kernel(*refs):
        del refs

    anywhere = pl.BlockSpec(memory_space=pl.ANY)
    return pl.pallas_call(
        kernel,
        out_shape=jax.ShapeDtypeStruct(array.shape, array.dtype),
        in_specs=[anywhere],
        out_specs=anywhere,
        input_output_aliases={0: 0},
        cost_estimate=pl.CostEstimate(flops=flops, bytes_accessed=0, transcendentals=0),
        compiler_params=pltpu.CompilerParams(vmem_limit_bytes=1 << 17),
        name="held",
    )(array)


def mirrored_groups(groups):
    def device(s, g, half, core):
        return ((s if half == 0 else 3 - s) * groups + g) * 4 + half * 2 + core

    return [
        [device(s, g, h, c) for g in range(groups) for h in range(2) for c in range(2)]
        for s in range(4)
    ]


def gated_rows_kernel(kind_ref, table_ref, ids_ref, index_ref, up_ref, out_ref):
    experts, tokens = out_ref.shape[0], up_ref.shape[0]
    width = out_ref.shape[2]
    ids, index = ids_ref[...], index_ref[...]
    expert = lax.broadcasted_iota(jnp.int32, (experts, tokens), 0)
    named = [ids[k : k + 1] == expert for k in range(2)]
    either = jnp.where(named[0] | named[1], 1.0, 0.0)
    before = lax.broadcasted_iota(jnp.int32, (tokens, tokens), 0) < lax.broadcasted_iota(
        jnp.int32, (tokens, tokens), 1
    )
    before = jnp.where(before, 1.0, 0.0).astype(jnp.bfloat16)
    earlier = jnp.dot(either.astype(jnp.bfloat16), before, preferred_element_type=jnp.float32)
    here = jnp.where(earlier == kind_ref[0].astype(jnp.float32), either, 0.0)
    gates = jnp.zeros(index.shape, jnp.float32)
    for level in range(table_ref.shape[0]):
        gates = jnp.where(index == level, table_ref[level], gates)
    gate = jnp.where(named[0], gates[0:1], gates[1:2]) * here
    row_gate = jnp.sum(gate, axis=1, keepdims=True)
    picked = jnp.dot(here.astype(jnp.bfloat16), up_ref[...], preferred_element_type=jnp.float32)
    rows = (row_gate * picked).astype(jnp.bfloat16)
    out_ref[:, 0, :] = rows[:, :width]
    out_ref[:, 1, :] = rows[:, width:]


def gated_rows(kind, table, ids, index, upstream, experts):
    smem = pl.BlockSpec(memory_space=pltpu.SMEM)
    vmem = pl.BlockSpec(memory_space=pltpu.VMEM)
    return pl.pallas_call(
        gated_rows_kernel,
        out_shape=jax.ShapeDtypeStruct((experts, 2, upstream.shape[1] // 2), jnp.bfloat16),
        in_specs=[smem, smem, vmem, vmem, vmem],
        out_specs=vmem,
        compiler_params=pltpu.CompilerParams(vmem_limit_bytes=8 << 20),
        name="gated_rows",
    )(kind.reshape(1), table, ids, index, upstream)


def reorder_kernel(section_ref, w_ref, after_ref, out_ref):
    del after_ref
    flipped = w_ref[...].T
    part = flipped.shape[0] // 4
    for j in range(4):
        to = pl.multiple_of(jnp.bitwise_xor(section_ref[0], j) * part, 32)
        out_ref[pl.ds(to, part), :] = flipped[j * part : (j + 1) * part]


def reorder(section, w, after):
    vmem = pl.BlockSpec(memory_space=pltpu.VMEM)
    return pl.pallas_call(
        reorder_kernel,
        out_shape=jax.ShapeDtypeStruct(w.shape[::-1], w.dtype),
        in_specs=[
            pl.BlockSpec(memory_space=pltpu.SMEM),
            vmem,
            pl.BlockSpec(memory_space=pl.ANY),
        ],
        out_specs=vmem,
        compiler_params=pltpu.CompilerParams(vmem_limit_bytes=8 << 20),
        name="reorder",
    )(section.reshape(1), w, after)


def ranks_of(flat_ids, tokens):
    pair = jnp.arange(flat_ids.shape[0], dtype=jnp.int32)
    token = jnp.where(pair >= tokens, pair - tokens, pair)
    same = (flat_ids[:, None] == flat_ids[None, :]) & (token[:, None] < token[None, :])
    return jnp.sum(same.astype(jnp.int32), axis=0)


def body(upstream, expert_ids, gate_index, gate_table, w_up, w_down, saved_pre):
    tokens, model_width = upstream.shape
    col_part = model_width // lax.axis_size("section")
    groups = lax.axis_size("expert")
    experts = groups * lax.axis_size("dp")
    capacity = saved_pre.shape[2]
    section = lax.axis_index("section")
    half = lax.axis_index("dp") // 2
    first = section % 2 == 0
    kind = jnp.where(first, half, 1 - half)

    flat_ids = expert_ids.T.reshape(-1)
    ranks = ranks_of(flat_ids, tokens)
    rows = gated_rows(kind, gate_table, expert_ids.T, gate_index.T, upstream, experts)
    arrived = lax.all_to_all(
        rows,
        ("section", "expert", "dp"),
        split_axis=0,
        concat_axis=0,
        axis_index_groups=mirrored_groups(groups),
        tiled=True,
    ).reshape(experts, model_width)

    weight_own = w_down[0]
    weight_other = held(lax.ppermute(weight_own, "section", NEAR), HELD_FLOPS)
    pre = saved_pre[0].transpose(1, 2, 0)
    pre_mine = jnp.where(kind == 0, pre[0], pre[1])
    pre_other = lax.ppermute(jnp.where(kind == 0, pre[1], pre[0]), "section", NEAR)

    def hidden_grad(weight, pre_act):
        proj = jnp.einsum("fd,sd->fs", weight, arrived, preferred_element_type=jnp.float32)
        pre_act = pre_act.astype(jnp.float32)
        sig = jax.nn.sigmoid(pre_act)
        return (proj * (sig * (1.0 + pre_act * (1.0 - sig)))).astype(jnp.bfloat16)

    hid_own = hidden_grad(weight_own, pre_mine)
    far_own = lax.ppermute(hid_own, "section", FAR)
    near_own = lax.ppermute(hid_own, "section", NEAR)
    hid_other = hidden_grad(weight_other, pre_other)
    far_other = lax.ppermute(hid_other, "section", FAR)
    near_other = lax.ppermute(hid_other, "section", NEAR)
    relay_own = lax.ppermute(far_own, "section", NEAR)
    relay_other = lax.ppermute(far_other, "section", NEAR)

    parts = reorder(section, w_up[0], hid_own)

    def back(pieces):
        out = jnp.einsum(
            "fs,fd->sd", jnp.concatenate(pieces), parts, preferred_element_type=jnp.float32
        )
        return out.astype(jnp.bfloat16)

    mine = back([hid_own, hid_other, far_own, far_other])
    theirs = back([near_other, near_own, relay_other, relay_own])
    back_rows = jnp.stack([mine, theirs], axis=1)
    returned = lax.all_to_all(
        back_rows, ("expert", "dp"), split_axis=0, concat_axis=0, tiled=True
    ).reshape(experts * capacity, col_part)

    sender_half = (flat_ids % 4) // 2
    served = jnp.where(first, sender_half, 1 - sender_half)
    places = flat_ids * capacity + jnp.where(ranks == served, 0, 1)
    wanted = places[:, None] == jnp.arange(experts * capacity, dtype=jnp.int32)
    wanted = (wanted[:tokens] | wanted[tokens:]).astype(jnp.bfloat16)
    total = jnp.dot(wanted, returned, preferred_element_type=jnp.float32)
    own_cols = lax.dynamic_slice_in_dim(upstream, section * col_part, col_part, 1)
    return (own_cols.astype(jnp.float32) + total).astype(jnp.bfloat16)


def solution(mesh):
    in_specs = (
        P(("expert", "dp"), None),
        P(("expert", "dp"), None),
        P(("expert", "dp"), None),
        P(),
        P(("expert", "dp"), "section", None),
        P(("expert", "dp"), "section", None),
        P(("expert", "dp"), None, None, "section"),
    )
    out_specs = P(("expert", "dp"), "section")
    return jax.shard_map(body, mesh=mesh, in_specs=in_specs, out_specs=out_specs, check_vma=False)
```

```python
import jax
import jax.numpy as jnp
from jax import lax
from jax.experimental import pallas as pl
from jax.experimental.pallas import tpu as pltpu
from jax.sharding import PartitionSpec as P

NEAR = [(0, 1), (1, 0), (2, 3), (3, 2)]
FAR = [(0, 2), (2, 0), (1, 3), (3, 1)]
HELD_FLOPS = 100_000_000_000
ROWS_VMEM = 65_200_000


def held(array, flops):
    def kernel(*refs):
        del refs

    anywhere = pl.BlockSpec(memory_space=pl.ANY)
    return pl.pallas_call(
        kernel,
        out_shape=jax.ShapeDtypeStruct(array.shape, array.dtype),
        in_specs=[anywhere],
        out_specs=anywhere,
        input_output_aliases={0: 0},
        cost_estimate=pl.CostEstimate(flops=flops, bytes_accessed=0, transcendentals=0),
        compiler_params=pltpu.CompilerParams(vmem_limit_bytes=1 << 17),
        name="held",
    )(array)


def mirrored_groups(groups):
    def device(s, g, half, core):
        return ((s if half == 0 else 3 - s) * groups + g) * 4 + half * 2 + core

    return [
        [device(s, g, h, c) for g in range(groups) for h in range(2) for c in range(2)]
        for s in range(4)
    ]


def gated_rows_kernel(kind_ref, table_ref, ids_ref, index_ref, up_ref, out_ref):
    experts, tokens = out_ref.shape[0], up_ref.shape[0]
    width = out_ref.shape[2]
    ids, index = ids_ref[...], index_ref[...]
    expert = lax.broadcasted_iota(jnp.int32, (experts, tokens), 0)
    named = [ids[k : k + 1] == expert for k in range(2)]
    either = jnp.where(named[0] | named[1], 1.0, 0.0)
    before = lax.broadcasted_iota(jnp.int32, (tokens, tokens), 0) < lax.broadcasted_iota(
        jnp.int32, (tokens, tokens), 1
    )
    before = jnp.where(before, 1.0, 0.0).astype(jnp.bfloat16)
    earlier = jnp.dot(either.astype(jnp.bfloat16), before, preferred_element_type=jnp.float32)
    here = jnp.where(earlier == kind_ref[0].astype(jnp.float32), either, 0.0)
    gates = jnp.zeros(index.shape, jnp.float32)
    for level in range(table_ref.shape[0]):
        gates = jnp.where(index == level, table_ref[level], gates)
    gate = jnp.where(named[0], gates[0:1], gates[1:2]) * here
    row_gate = jnp.sum(gate, axis=1, keepdims=True)
    picked = jnp.dot(here.astype(jnp.bfloat16), up_ref[...], preferred_element_type=jnp.float32)
    rows = (row_gate * picked).astype(jnp.bfloat16)
    out_ref[:, 0, :] = rows[:, :width]
    out_ref[:, 1, :] = rows[:, width:]


def gated_rows(kind, table, ids, index, upstream, experts):
    smem = pl.BlockSpec(memory_space=pltpu.SMEM)
    vmem = pl.BlockSpec(memory_space=pltpu.VMEM)
    return pl.pallas_call(
        gated_rows_kernel,
        out_shape=jax.ShapeDtypeStruct((experts, 2, upstream.shape[1] // 2), jnp.bfloat16),
        in_specs=[smem, smem, vmem, vmem, vmem],
        out_specs=vmem,
        compiler_params=pltpu.CompilerParams(vmem_limit_bytes=ROWS_VMEM),
        name="gated_rows",
    )(kind.reshape(1), table, ids, index, upstream)


def reorder_kernel(section_ref, w_ref, after_ref, out_ref):
    del after_ref
    flipped = w_ref[...].T
    part = flipped.shape[0] // 4
    for j in range(4):
        to = pl.multiple_of(jnp.bitwise_xor(section_ref[0], j) * part, 32)
        out_ref[pl.ds(to, part), :] = flipped[j * part : (j + 1) * part]


def reorder(section, w, after):
    vmem = pl.BlockSpec(memory_space=pltpu.VMEM)
    return pl.pallas_call(
        reorder_kernel,
        out_shape=jax.ShapeDtypeStruct(w.shape[::-1], w.dtype),
        in_specs=[
            pl.BlockSpec(memory_space=pltpu.SMEM),
            vmem,
            pl.BlockSpec(memory_space=pl.ANY),
        ],
        out_specs=vmem,
        compiler_params=pltpu.CompilerParams(vmem_limit_bytes=8 << 20),
        name="reorder",
    )(section.reshape(1), w, after)


def ranks_of(flat_ids, tokens):
    pair = jnp.arange(flat_ids.shape[0], dtype=jnp.int32)
    token = jnp.where(pair >= tokens, pair - tokens, pair)
    same = (flat_ids[:, None] == flat_ids[None, :]) & (token[:, None] < token[None, :])
    return jnp.sum(same.astype(jnp.int32), axis=0)


def body(upstream, expert_ids, gate_index, gate_table, w_up, w_down, saved_pre):
    tokens, model_width = upstream.shape
    col_part = model_width // lax.axis_size("section")
    groups = lax.axis_size("expert")
    experts = groups * lax.axis_size("dp")
    capacity = saved_pre.shape[2]
    section = lax.axis_index("section")
    half = lax.axis_index("dp") // 2
    first = section % 2 == 0
    kind = jnp.where(first, half, 1 - half)

    flat_ids = expert_ids.T.reshape(-1)
    ranks = ranks_of(flat_ids, tokens)
    rows = gated_rows(kind, gate_table, expert_ids.T, gate_index.T, upstream, experts)
    arrived = lax.all_to_all(
        rows,
        ("section", "expert", "dp"),
        split_axis=0,
        concat_axis=0,
        axis_index_groups=mirrored_groups(groups),
        tiled=True,
    ).reshape(experts, model_width)

    weight_own = w_down[0]
    weight_other = held(lax.ppermute(weight_own, "section", NEAR), HELD_FLOPS)
    pre = saved_pre[0].transpose(1, 2, 0)
    pre_mine = jnp.where(kind == 0, pre[0], pre[1])
    pre_other = lax.ppermute(jnp.where(kind == 0, pre[1], pre[0]), "section", NEAR)

    def hidden_grad(weight, pre_act):
        proj = jnp.einsum("fd,sd->fs", weight, arrived, preferred_element_type=jnp.float32)
        pre_act = pre_act.astype(jnp.float32)
        sig = jax.nn.sigmoid(pre_act)
        return (proj * (sig * (1.0 + pre_act * (1.0 - sig)))).astype(jnp.bfloat16)

    hid_own = hidden_grad(weight_own, pre_mine)
    far_own = lax.ppermute(hid_own, "section", FAR)
    hid_other = hidden_grad(weight_other, pre_other)
    far_other = lax.ppermute(hid_other, "section", FAR)
    near = lax.ppermute(jnp.concatenate([hid_other, hid_own]), "section", NEAR)
    relay_own = lax.ppermute(far_own, "section", NEAR)
    relay_other = lax.ppermute(far_other, "section", NEAR)

    parts = reorder(section, w_up[0], hid_own)

    def back(pieces):
        out = jnp.einsum(
            "fs,fd->sd", jnp.concatenate(pieces), parts, preferred_element_type=jnp.float32
        )
        return out.astype(jnp.bfloat16)

    mine = back([hid_own, hid_other, far_own, far_other])
    theirs = back([near, relay_other, relay_own])
    back_rows = jnp.stack([mine, theirs], axis=1)
    returned = lax.all_to_all(
        back_rows, ("expert", "dp"), split_axis=0, concat_axis=0, tiled=True
    ).reshape(experts * capacity, col_part)

    sender_half = (flat_ids % 4) // 2
    served = jnp.where(first, sender_half, 1 - sender_half)
    places = flat_ids * capacity + jnp.where(ranks == served, 0, 1)
    wanted = places[:, None] == jnp.arange(experts * capacity, dtype=jnp.int32)
    wanted = (wanted[:tokens] | wanted[tokens:]).astype(jnp.bfloat16)
    own_cols = lax.dynamic_slice_in_dim(upstream, section * col_part, col_part, 1)
    wanted, own_cols = lax.optimization_barrier((wanted, own_cols))
    total = jnp.dot(wanted, returned, preferred_element_type=jnp.float32)
    return (own_cols.astype(jnp.float32) + total).astype(jnp.bfloat16)


def solution(mesh):
    in_specs = (
        P(("expert", "dp"), None),
        P(("expert", "dp"), None),
        P(("expert", "dp"), None),
        P(),
        P(("expert", "dp"), "section", None),
        P(("expert", "dp"), "section", None),
        P(("expert", "dp"), None, None, "section"),
    )
    out_specs = P(("expert", "dp"), "section")
    return jax.shard_map(body, mesh=mesh, in_specs=in_specs, out_specs=out_specs, check_vma=False)
```

```python
import jax
import jax.numpy as jnp
from jax import lax
from jax.experimental import pallas as pl
from jax.experimental.pallas import tpu as pltpu
from jax.sharding import PartitionSpec as P

NEAR = [(0, 1), (1, 0), (2, 3), (3, 2)]
FAR = [(0, 2), (2, 0), (1, 3), (3, 1)]
DIAGONAL = [(0, 3), (3, 0), (1, 2), (2, 1)]
HELD_FLOPS = 100_000_000_000
ROWS_VMEM = 65_200_000


def held(array, flops):
    def kernel(*refs):
        del refs

    anywhere = pl.BlockSpec(memory_space=pl.ANY)
    return pl.pallas_call(
        kernel,
        out_shape=jax.ShapeDtypeStruct(array.shape, array.dtype),
        in_specs=[anywhere],
        out_specs=anywhere,
        input_output_aliases={0: 0},
        cost_estimate=pl.CostEstimate(flops=flops, bytes_accessed=0, transcendentals=0),
        compiler_params=pltpu.CompilerParams(vmem_limit_bytes=1 << 17),
        name="held",
    )(array)


def mirrored_groups(groups):
    def device(s, g, half, core):
        return ((s if half == 0 else 3 - s) * groups + g) * 4 + half * 2 + core

    return [
        [device(s, g, h, c) for g in range(groups) for h in range(2) for c in range(2)]
        for s in range(4)
    ]


def gated_rows_kernel(kind_ref, table_ref, ids_ref, index_ref, up_ref, out_ref):
    experts, tokens = out_ref.shape[0], up_ref.shape[0]
    width = out_ref.shape[2]
    ids, index = ids_ref[...], index_ref[...]
    expert = lax.broadcasted_iota(jnp.int32, (experts, tokens), 0)
    named = [ids[k : k + 1] == expert for k in range(2)]
    either = jnp.where(named[0] | named[1], 1.0, 0.0)
    before = lax.broadcasted_iota(jnp.int32, (tokens, tokens), 0) < lax.broadcasted_iota(
        jnp.int32, (tokens, tokens), 1
    )
    before = jnp.where(before, 1.0, 0.0).astype(jnp.bfloat16)
    earlier = jnp.dot(either.astype(jnp.bfloat16), before, preferred_element_type=jnp.float32)
    here = jnp.where(earlier == kind_ref[0].astype(jnp.float32), either, 0.0)
    gates = jnp.zeros(index.shape, jnp.float32)
    for level in range(table_ref.shape[0]):
        gates = jnp.where(index == level, table_ref[level], gates)
    gate = jnp.where(named[0], gates[0:1], gates[1:2]) * here
    row_gate = jnp.sum(gate, axis=1, keepdims=True)
    picked = jnp.dot(here.astype(jnp.bfloat16), up_ref[...], preferred_element_type=jnp.float32)
    rows = (row_gate * picked).astype(jnp.bfloat16)
    out_ref[:, 0, :] = rows[:, :width]
    out_ref[:, 1, :] = rows[:, width:]


def gated_rows(kind, table, ids, index, upstream, experts):
    smem = pl.BlockSpec(memory_space=pltpu.SMEM)
    vmem = pl.BlockSpec(memory_space=pltpu.VMEM)
    return pl.pallas_call(
        gated_rows_kernel,
        out_shape=jax.ShapeDtypeStruct((experts, 2, upstream.shape[1] // 2), jnp.bfloat16),
        in_specs=[smem, smem, vmem, vmem, vmem],
        out_specs=vmem,
        compiler_params=pltpu.CompilerParams(vmem_limit_bytes=ROWS_VMEM),
        name="gated_rows",
    )(kind.reshape(1), table, ids, index, upstream)


def reorder_kernel(section_ref, w_ref, after_ref, out_ref):
    del after_ref
    flipped = w_ref[...].T
    part = flipped.shape[0] // 4
    for j in range(4):
        to = pl.multiple_of(jnp.bitwise_xor(section_ref[0], j) * part, 32)
        out_ref[pl.ds(to, part), :] = flipped[j * part : (j + 1) * part]


def reorder(section, w, after):
    vmem = pl.BlockSpec(memory_space=pltpu.VMEM)
    return pl.pallas_call(
        reorder_kernel,
        out_shape=jax.ShapeDtypeStruct(w.shape[::-1], w.dtype),
        in_specs=[
            pl.BlockSpec(memory_space=pltpu.SMEM),
            vmem,
            pl.BlockSpec(memory_space=pl.ANY),
        ],
        out_specs=vmem,
        compiler_params=pltpu.CompilerParams(vmem_limit_bytes=8 << 20),
        name="reorder",
    )(section.reshape(1), w, after)


def ranks_of(flat_ids, tokens):
    pair = jnp.arange(flat_ids.shape[0], dtype=jnp.int32)
    token = jnp.where(pair >= tokens, pair - tokens, pair)
    same = (flat_ids[:, None] == flat_ids[None, :]) & (token[:, None] < token[None, :])
    return jnp.sum(same.astype(jnp.int32), axis=0)


def body(upstream, expert_ids, gate_index, gate_table, w_up, w_down, saved_pre):
    tokens, model_width = upstream.shape
    col_part = model_width // lax.axis_size("section")
    groups = lax.axis_size("expert")
    experts = groups * lax.axis_size("dp")
    capacity = saved_pre.shape[2]
    section = lax.axis_index("section")
    half = lax.axis_index("dp") // 2
    first = section % 2 == 0
    kind = jnp.where(first, half, 1 - half)

    flat_ids = expert_ids.T.reshape(-1)
    ranks = ranks_of(flat_ids, tokens)
    rows = gated_rows(kind, gate_table, expert_ids.T, gate_index.T, upstream, experts)
    arrived = lax.all_to_all(
        rows,
        ("section", "expert", "dp"),
        split_axis=0,
        concat_axis=0,
        axis_index_groups=mirrored_groups(groups),
        tiled=True,
    ).reshape(experts, model_width)

    weight_own = w_down[0]
    weight_other = held(lax.ppermute(weight_own, "section", NEAR), HELD_FLOPS)
    pre = saved_pre[0].transpose(1, 2, 0)
    pre_mine = jnp.where(kind == 0, pre[0], pre[1])
    pre_other = lax.ppermute(jnp.where(kind == 0, pre[1], pre[0]), "section", NEAR)

    def hidden_grad(weight, pre_act):
        proj = jnp.einsum("fd,sd->fs", weight, arrived, preferred_element_type=jnp.float32)
        pre_act = pre_act.astype(jnp.float32)
        sig = jax.nn.sigmoid(pre_act)
        return (proj * (sig * (1.0 + pre_act * (1.0 - sig)))).astype(jnp.bfloat16)

    hid_other = hidden_grad(weight_other, pre_other)
    far_other = lax.ppermute(hid_other, "section", FAR)
    weight_own, hid_other = lax.optimization_barrier((weight_own, hid_other))
    hid_own = hidden_grad(weight_own, pre_mine)
    far_own = lax.ppermute(hid_own, "section", FAR)
    near = lax.ppermute(jnp.concatenate([hid_other, hid_own]), "section", NEAR)
    diagonal_own = lax.ppermute(hid_own, "section", DIAGONAL)
    relay_other = lax.ppermute(far_other, "section", NEAR)

    parts = reorder(section, w_up[0], hid_own)

    def back(pieces):
        out = jnp.einsum(
            "fs,fd->sd", jnp.concatenate(pieces), parts, preferred_element_type=jnp.float32
        )
        return out.astype(jnp.bfloat16)

    mine = back([hid_own, hid_other, far_own, far_other])
    theirs = back([near, relay_other, diagonal_own])
    back_rows = jnp.stack([mine, theirs], axis=1)
    returned = lax.all_to_all(
        back_rows, ("expert", "dp"), split_axis=0, concat_axis=0, tiled=True
    ).reshape(experts * capacity, col_part)

    sender_half = (flat_ids % 4) // 2
    served = jnp.where(first, sender_half, 1 - sender_half)
    places = flat_ids * capacity + jnp.where(ranks == served, 0, 1)
    wanted = places[:, None] == jnp.arange(experts * capacity, dtype=jnp.int32)
    wanted = (wanted[:tokens] | wanted[tokens:]).astype(jnp.bfloat16)
    own_cols = lax.dynamic_slice_in_dim(upstream, section * col_part, col_part, 1)
    wanted, own_cols = lax.optimization_barrier((wanted, own_cols))
    total = jnp.dot(wanted, returned, preferred_element_type=jnp.float32)
    return (own_cols.astype(jnp.float32) + total).astype(jnp.bfloat16)


def solution(mesh):
    in_specs = (
        P(("expert", "dp"), None),
        P(("expert", "dp"), None),
        P(("expert", "dp"), None),
        P(),
        P(("expert", "dp"), "section", None),
        P(("expert", "dp"), "section", None),
        P(("expert", "dp"), None, None, "section"),
    )
    out_specs = P(("expert", "dp"), "section")
    return jax.shard_map(body, mesh=mesh, in_specs=in_specs, out_specs=out_specs, check_vma=False)
```

```python
import jax
import jax.numpy as jnp
from jax import lax
from jax.experimental import pallas as pl
from jax.experimental.pallas import tpu as pltpu
from jax.sharding import PartitionSpec as P

NEAR = [(0, 1), (1, 0), (2, 3), (3, 2)]
FAR = [(0, 2), (2, 0), (1, 3), (3, 1)]
DIAGONAL = [(0, 3), (3, 0), (1, 2), (2, 1)]
HELD_FLOPS = 100_000_000_000
ROWS_VMEM = 65_200_000


def held(array, flops):
    def kernel(*refs):
        del refs

    anywhere = pl.BlockSpec(memory_space=pl.ANY)
    return pl.pallas_call(
        kernel,
        out_shape=jax.ShapeDtypeStruct(array.shape, array.dtype),
        in_specs=[anywhere],
        out_specs=anywhere,
        input_output_aliases={0: 0},
        cost_estimate=pl.CostEstimate(flops=flops, bytes_accessed=0, transcendentals=0),
        compiler_params=pltpu.CompilerParams(vmem_limit_bytes=1 << 17),
        name="held",
    )(array)


def mirrored_groups(groups):
    def device(s, g, half, core):
        return ((s if half == 0 else 3 - s) * groups + g) * 4 + half * 2 + core

    return [
        [device(s, g, h, c) for g in range(groups) for h in range(2) for c in range(2)]
        for s in range(4)
    ]


def gated_rows_kernel(kind_ref, table_ref, ids_ref, index_ref, up_ref, out_ref):
    experts, tokens = out_ref.shape[0], up_ref.shape[0]
    width = out_ref.shape[2]
    ids, index = ids_ref[...], index_ref[...]
    expert = lax.broadcasted_iota(jnp.int32, (experts, tokens), 0)
    named = [ids[k : k + 1] == expert for k in range(2)]
    either = jnp.where(named[0] | named[1], 1.0, 0.0)
    before = lax.broadcasted_iota(jnp.int32, (tokens, tokens), 0) < lax.broadcasted_iota(
        jnp.int32, (tokens, tokens), 1
    )
    before = jnp.where(before, 1.0, 0.0).astype(jnp.bfloat16)
    earlier = jnp.dot(either.astype(jnp.bfloat16), before, preferred_element_type=jnp.float32)
    here = jnp.where(earlier == kind_ref[0].astype(jnp.float32), either, 0.0)
    gates = jnp.zeros(index.shape, jnp.float32)
    for level in range(table_ref.shape[0]):
        gates = jnp.where(index == level, table_ref[level], gates)
    gate = jnp.where(named[0], gates[0:1], gates[1:2]) * here
    row_gate = jnp.sum(gate, axis=1, keepdims=True)
    picked = jnp.dot(here.astype(jnp.bfloat16), up_ref[...], preferred_element_type=jnp.float32)
    rows = (row_gate * picked).astype(jnp.bfloat16)
    out_ref[:, 0, :] = rows[:, :width]
    out_ref[:, 1, :] = rows[:, width:]


def gated_rows(kind, table, ids, index, upstream, experts):
    smem = pl.BlockSpec(memory_space=pltpu.SMEM)
    vmem = pl.BlockSpec(memory_space=pltpu.VMEM)
    return pl.pallas_call(
        gated_rows_kernel,
        out_shape=jax.ShapeDtypeStruct((experts, 2, upstream.shape[1] // 2), jnp.bfloat16),
        in_specs=[smem, smem, vmem, vmem, vmem],
        out_specs=vmem,
        compiler_params=pltpu.CompilerParams(vmem_limit_bytes=ROWS_VMEM),
        name="gated_rows",
    )(kind.reshape(1), table, ids, index, upstream)


def join_kernel(mine_ref, near_ref, diagonal_ref, relay_ref, w_ref, out_ref):
    total, at = None, 0
    for piece in (near_ref, diagonal_ref, relay_ref):
        depth = piece.shape[0]
        term = lax.dot_general(
            piece[...],
            w_ref[at : at + depth],
            (((0,), (0,)), ((), ())),
            preferred_element_type=jnp.float32,
        )
        total, at = term if total is None else total + term, at + depth
    out_ref[:, 0, :] = mine_ref[...]
    out_ref[:, 1, :] = total.astype(out_ref.dtype)


def join(mine, near, diagonal, relay, w):
    vmem = pl.BlockSpec(memory_space=pltpu.VMEM)
    return pl.pallas_call(
        join_kernel,
        out_shape=jax.ShapeDtypeStruct((mine.shape[0], 2, mine.shape[1]), mine.dtype),
        in_specs=[vmem] * 5,
        out_specs=vmem,
        compiler_params=pltpu.CompilerParams(vmem_limit_bytes=8 << 20),
        name="join",
    )(mine, near, diagonal, relay, w)


def reorder_kernel(section_ref, w_ref, after_ref, out_ref):
    del after_ref
    flipped = w_ref[...].T
    part = flipped.shape[0] // 4
    for j in range(4):
        to = pl.multiple_of(jnp.bitwise_xor(section_ref[0], j) * part, 32)
        out_ref[pl.ds(to, part), :] = flipped[j * part : (j + 1) * part]


def reorder(section, w, after):
    vmem = pl.BlockSpec(memory_space=pltpu.VMEM)
    return pl.pallas_call(
        reorder_kernel,
        out_shape=jax.ShapeDtypeStruct(w.shape[::-1], w.dtype),
        in_specs=[
            pl.BlockSpec(memory_space=pltpu.SMEM),
            vmem,
            pl.BlockSpec(memory_space=pl.ANY),
        ],
        out_specs=vmem,
        compiler_params=pltpu.CompilerParams(vmem_limit_bytes=8 << 20),
        name="reorder",
    )(section.reshape(1), w, after)


def ranks_of(flat_ids, tokens):
    pair = jnp.arange(flat_ids.shape[0], dtype=jnp.int32)
    token = jnp.where(pair >= tokens, pair - tokens, pair)
    same = (flat_ids[:, None] == flat_ids[None, :]) & (token[:, None] < token[None, :])
    return jnp.sum(same.astype(jnp.int32), axis=0)


def body(upstream, expert_ids, gate_index, gate_table, w_up, w_down, saved_pre):
    tokens, model_width = upstream.shape
    col_part = model_width // lax.axis_size("section")
    groups = lax.axis_size("expert")
    experts = groups * lax.axis_size("dp")
    capacity = saved_pre.shape[2]
    section = lax.axis_index("section")
    half = lax.axis_index("dp") // 2
    first = section % 2 == 0
    kind = jnp.where(first, half, 1 - half)

    flat_ids = expert_ids.T.reshape(-1)
    ranks = ranks_of(flat_ids, tokens)
    rows = gated_rows(kind, gate_table, expert_ids.T, gate_index.T, upstream, experts)
    arrived = lax.all_to_all(
        rows,
        ("section", "expert", "dp"),
        split_axis=0,
        concat_axis=0,
        axis_index_groups=mirrored_groups(groups),
        tiled=True,
    ).reshape(experts, model_width)

    weight_own = w_down[0]
    weight_other = held(lax.ppermute(weight_own, "section", NEAR), HELD_FLOPS)
    pre = saved_pre[0].transpose(1, 2, 0)
    pre_mine = jnp.where(kind == 0, pre[0], pre[1])
    pre_other = lax.ppermute(jnp.where(kind == 0, pre[1], pre[0]), "section", NEAR)

    def hidden_grad(weight, pre_act):
        proj = jnp.einsum("fd,sd->fs", weight, arrived, preferred_element_type=jnp.float32)
        pre_act = pre_act.astype(jnp.float32)
        sig = jax.nn.sigmoid(pre_act)
        return (proj * (sig * (1.0 + pre_act * (1.0 - sig)))).astype(jnp.bfloat16)

    hid_own = hidden_grad(weight_own, pre_mine)
    far_own = lax.ppermute(hid_own, "section", FAR)
    pre_other, weight_other, hid_own = lax.optimization_barrier((pre_other, weight_other, hid_own))
    hid_other = hidden_grad(weight_other, pre_other)
    near = lax.ppermute(jnp.concatenate([hid_other, hid_own]), "section", NEAR)
    far_other = lax.ppermute(hid_other, "section", FAR)
    diagonal_other = lax.ppermute(hid_other, "section", DIAGONAL)
    relay_own = lax.ppermute(far_own, "section", NEAR)

    parts = reorder(section, w_up[0], hid_own)

    def back(pieces):
        out = jnp.einsum(
            "fs,fd->sd", jnp.concatenate(pieces), parts, preferred_element_type=jnp.float32
        )
        return out.astype(jnp.bfloat16)

    mine = back([hid_own, hid_other, far_own, far_other])
    back_rows = join(mine, near, diagonal_other, relay_own, parts)
    returned = lax.all_to_all(
        back_rows, ("expert", "dp"), split_axis=0, concat_axis=0, tiled=True
    ).reshape(experts * capacity, col_part)

    sender_half = (flat_ids % 4) // 2
    served = jnp.where(first, sender_half, 1 - sender_half)
    places = flat_ids * capacity + jnp.where(ranks == served, 0, 1)
    wanted = places[:, None] == jnp.arange(experts * capacity, dtype=jnp.int32)
    wanted = (wanted[:tokens] | wanted[tokens:]).astype(jnp.bfloat16)
    own_cols = lax.dynamic_slice_in_dim(upstream, section * col_part, col_part, 1)
    wanted, own_cols = lax.optimization_barrier((wanted, own_cols))
    total = jnp.dot(wanted, returned, preferred_element_type=jnp.float32)
    return (own_cols.astype(jnp.float32) + total).astype(jnp.bfloat16)


def solution(mesh):
    in_specs = (
        P(("expert", "dp"), None),
        P(("expert", "dp"), None),
        P(("expert", "dp"), None),
        P(),
        P(("expert", "dp"), "section", None),
        P(("expert", "dp"), "section", None),
        P(("expert", "dp"), None, None, "section"),
    )
    out_specs = P(("expert", "dp"), "section")
    return jax.shard_map(body, mesh=mesh, in_specs=in_specs, out_specs=out_specs, check_vma=False)
```
